32 devices in a mesh: grp: 4 (over y, core), row: 8 (over z, x).
Axes of the slice: x: 2, y: 2, z: 4, core: 2. Of those that a mesh axis runs over, the one named last changes fastest.
Arguments:
- grad: float32 [32, 2048, 512], P('grp', 'row')
- weight: bfloat16 [32, 2048, 512], P('grp', 'row'), may hold values from -0.125 to 0.125
- owner: int32 [32, 1], P('grp'), may hold values from 0 to 7; in each aligned block of 8 rows (0 to 7, 8 to 15, ...) at most 2 rows name the same one
- tokens: bfloat16 [3072, 2048], P('row'), may hold values from -6 to 6
- counts: int32 [8], P('row'), may hold values from 96 to 384, as said below
Outputs:
- new_weight: bfloat16 [32, 2048, 512], P('grp', 'row')
- mixed: bfloat16 [3072, 512], P('row', 'grp')
The draws below stay inside these ranges and needn't reach their ends.
Inputs may be any that keep to these rules, and one draw needn't show every extreme that they name: Within each group's 8 consecutive matrices no owner is named more than 2 times, a bound that some block reaches. `counts`: some row index has all 384 rows live.
All inputs are finite; a program needn't handle non-finite values.
Results may differ from the reference program's by a relative error of at most 0.017.
Values may be sent and summed in bfloat16 or wider, within the bound.
A program may use at most 128 MiB of HBM per device.

```python
import math
import jax
import jax.numpy as jnp
import numpy as np
from jax import lax

H = 2048
F = 512
TOK_DEV = 384
ITERS = 5
MOST = 2
EXP_G = 8
EXPERTS = 32
TOKENS = 3072
N_GRP = 4
N_ROW = 8


def draw_grad(key, part):
    keys = jax.random.split(jax.random.fold_in(key, 11), 3)
    shape = (EXPERTS, H, F)
    base = jax.random.normal(keys[0], shape, jnp.float32)
    row_scale = jnp.exp(jax.random.uniform(keys[1], (EXPERTS, H, 1), jnp.float32) * math.log(10.0))
    rising = jnp.exp(math.log(3.0) * jnp.arange(H, dtype=jnp.float32) / H)[None, :, None]
    col_scale = jnp.exp(jax.random.uniform(keys[2], (EXPERTS, 1, F), jnp.float32) * math.log(10.0))
    return base * row_scale * rising * col_scale


def draw_counts(key, part):
    keys = jax.random.split(jax.random.fold_in(key, 23), 2)
    values = jax.random.randint(keys[0], (N_ROW,), TOK_DEV // 4, TOK_DEV + 1)
    chosen = jax.random.randint(keys[1], (), 0, N_ROW)
    return jnp.where(jnp.arange(N_ROW) == chosen, TOK_DEV, values).astype(jnp.int32)


def block_scale(rng, dims, shards, least, largest):
    gain, own = 1.0, jax.random.fold_in(rng, 6)
    for position, shards_of in shards:
        steps = jnp.exp(jax.random.uniform(jax.random.fold_in(own, position), (shards_of,), jnp.float32, least / len(shards), largest / len(shards)))
        gain = gain * jnp.repeat(steps, dims[position] // shards_of).reshape([-1 if axis == position else 1 for axis in range(len(dims))])
    return gain


def routed_block(rng, own, number, rows, number_of, top, bound, slope):
    order = jax.random.permutation(rng, number_of)
    crowded, usual = portions_of(number_of, rows * top, bound, slope, True), portions_of(number_of, rows * top, bound, slope, False)
    places = jnp.arange(number_of)

    def named(sizes, turn):
        used = int((sizes > 0).sum())
        fixed = max(1, used // 4)
        passed = fixed + (places - fixed + turn * (used - fixed)) % max(1, number_of - fixed)
        return jnp.zeros((number_of,), jnp.int32).at[order[jnp.where(places < fixed, places, passed)]].set(jnp.asarray(sizes, jnp.int32))

    sizes = jnp.where(number % 4 == 0, named(crowded, number // 4), named(usual, number - number // 4 - 1))
    mixed = jax.random.permutation(jax.random.fold_in(own, 3), number_of)
    giver, sink = mixed[0:number_of // 2 * 2:2], mixed[1:number_of // 2 * 2:2]
    slack = jnp.minimum(sizes[giver] - 1, bound - sizes[sink]) // 2
    slack = jnp.where((giver == order[0]) | (sink == order[0]) | (sizes[sink] == 0), 0, jnp.maximum(slack, 0))
    passed = jax.random.randint(jax.random.fold_in(own, 4), (number_of // 2,), 0, 1 << 20) % (slack + 1)
    sizes = sizes.at[giver].add(-passed).at[sink].add(passed)
    labels = jnp.searchsorted(jnp.cumsum(sizes), jnp.arange(rows * top), side="right").astype(jnp.int32)
    grid = labels.reshape(top, rows).T
    grid = grid[jax.random.permutation(jax.random.fold_in(own, 1), rows)]
    turn = jax.random.randint(jax.random.fold_in(own, 2), (rows, 1), 0, top)
    return jnp.take_along_axis(grid, (jnp.arange(top)[None, :] + turn) % top, axis=1)


def portions_of(number_of, total, bound, slope, full):
    loads = [(1 << 20) // math.isqrt(grade ** slope) + 1 for grade in range(1, number_of + 1)]
    largest = bound if full else min(bound, max(-(-total // number_of), total * loads[0] // sum(loads)))
    least = 1 if total - largest >= number_of - 1 else 0
    given, spare = [largest] + [least] * (number_of - 1), total - largest - least * (number_of - 1)
    while spare > 0:
        free = [i for i in range(1, number_of) if given[i] < largest] or [i for i in range(1, number_of) if given[i] < bound]
        pool, left = sum([loads[i] for i in free]), spare
        for i in free:
            extra = min(bound - given[i], max(1, left * loads[i] // pool), spare)
            given[i] = given[i] + extra
            spare = spare - extra
    return np.array(given)


def gaussian(key, dims, spread, reach, shards=(), held_as=jnp.bfloat16):
    result = spread * jax.random.normal(key, dims, jnp.float32)
    if shards:
        result = result * block_scale(key, dims, shards, -0.22, 0.18)
    return jnp.clip(result, -reach, reach).astype(held_as)


def setup_inputs(seed: int = 0) -> dict:
    splits = jax.random.split(jax.random.key(seed), 6)
    grad = draw_grad(jax.random.fold_in(splits[5], 71), 0)
    weight = gaussian(splits[1], (EXPERTS, H, F), H ** -0.5, 0.125, ((0, 4), (1, 8)))
    owner_keys = jax.random.split(jax.random.fold_in(splits[2], 1), EXPERTS // EXP_G)
    owner_turns = jax.random.permutation(jax.random.fold_in(splits[2], 3), EXPERTS // EXP_G)
    owner = jax.vmap(lambda own, number: routed_block(jax.random.fold_in(splits[2], 2), own, number, EXP_G, N_ROW, 1, MOST, 2))(owner_keys, owner_turns).reshape((EXPERTS, 1))
    tokens = gaussian(splits[3], (TOKENS, H), 1.0, 6.0, ((0, 8),))
    counts = draw_counts(jax.random.fold_in(splits[5], 71), 0)
    return {"grad": grad, "weight": weight, "owner": owner, "tokens": tokens, "counts": counts}


coef_a = 3.4445
coef_b = -4.775
coef_c = 2.0315
step_size = 0.5

def newton_schulz(start):
    iterate_state = start
    for turn in range(ITERS):
        gram_product = jnp.dot(iterate_state.T, iterate_state, preferred_element_type=jnp.float32).astype(jnp.bfloat16)
        square = jnp.dot(gram_product, gram_product, preferred_element_type=jnp.float32)
        polynomial_term = (coef_b * gram_product.astype(jnp.float32) + coef_c * square).astype(jnp.bfloat16)
        iterate_state = (coef_a * iterate_state.astype(jnp.float32) + jnp.dot(iterate_state, polynomial_term, preferred_element_type=jnp.float32)).astype(jnp.bfloat16)
    return iterate_state

def reference(grad, weight, owner, tokens, counts):
    norm2 = lax.optimization_barrier(jnp.sum(grad * grad, axis=(1, 2)))
    start = (grad / (jnp.sqrt(norm2) + 1e-07)[:, None, None]).astype(jnp.bfloat16)
    blocks = tokens.reshape(N_ROW, TOK_DEV, H)

    def turn_one(total, item):
        matrix, old, target = item
        ortho = newton_schulz(matrix)
        recent_matrix = (old.astype(jnp.float32) - step_size * ortho.astype(jnp.float32)).astype(jnp.bfloat16)
        rows_in = lax.dynamic_index_in_dim(blocks, target, 0, keepdims=False)
        term = jnp.dot(rows_in, recent_matrix, preferred_element_type=jnp.float32)
        total = total.at[target].add(term)
        return (total, recent_matrix)
    initial_total0 = jnp.zeros((N_ROW, TOK_DEV, F), jnp.float32)
    total, new_weight = lax.scan(turn_one, initial_total0, (start, weight, owner[:, 0].astype(jnp.int32)))
    proj = total * N_GRP ** (-0.5)
    live = jnp.arange(TOK_DEV)[None, :, None] < counts[:, None, None]
    mixed = jnp.where(live, proj, 0.0).reshape(N_ROW * TOK_DEV, F).astype(jnp.bfloat16)
    return (new_weight, mixed)
```

```python
import jax
import jax.numpy as jnp
from jax import lax
from jax.sharding import PartitionSpec as P

ITERS = 5
MOST = 2

coef_a = 3.4445
coef_b = -4.775
coef_c = 2.0315
step_size = 0.5

f32 = jnp.float32
bf16 = jnp.bfloat16


def newton_schulz(raw):
    x32 = raw.astype(f32)
    norm2 = jnp.sum(x32 * x32)
    scale = 1.0 / (jnp.sqrt(norm2) + 1e-07)
    state = raw
    for turn in range(ITERS):
        gram = jnp.dot(state.T, state, preferred_element_type=f32)
        if turn == 0:
            gram = jnp.where(norm2 < jnp.inf, scale * (scale * gram), 0.0)
        gram = gram.astype(bf16)
        square = jnp.dot(gram, gram, preferred_element_type=f32)
        poly = (coef_b * gram.astype(f32) + coef_c * square).astype(bf16)
        update = jnp.dot(state, poly, preferred_element_type=f32)
        if turn == 0:
            state = ((coef_a * scale) * state.astype(f32) + scale * update).astype(bf16)
        else:
            state = (coef_a * state.astype(f32) + update).astype(bf16)
    return state


def body(grad, weight, owner, tokens, counts):
    ranks = lax.axis_size("row")
    groups = lax.axis_size("grp")
    number, rows, width = grad.shape
    top = float(jnp.finfo(bf16).max)
    raw = jnp.clip(grad, -top, top).astype(bf16)
    assert number == ranks
    whole = lax.all_to_all(raw, "row", split_axis=0, concat_axis=0, tiled=True)

    count = tokens.shape[0]
    part = count // groups
    mine = lax.dynamic_slice_in_dim(tokens, lax.axis_index("grp") * part, part, 0)
    mine = mine.reshape(part, ranks, rows).transpose(1, 0, 2)
    moved = lax.all_to_all(mine, "row", split_axis=0, concat_axis=0, tiled=True)
    cols = lax.all_gather(moved, "grp", axis=1, tiled=True)

    ortho = newton_schulz(whole.reshape(ranks * rows, width))
    back = lax.all_to_all(
        ortho.reshape(ranks, rows, width), "row", split_axis=0, concat_axis=0, tiled=True
    )
    new_weight = (weight.astype(f32) - step_size * back.astype(f32)).astype(bf16)

    target = owner[:, 0]
    before = jnp.arange(number)[None, :] < jnp.arange(number)[:, None]
    same = target[None, :] == target[:, None]
    slot = jnp.sum((same & before).astype(jnp.int32), axis=1)
    hit = (target[None, None, :] == jnp.arange(ranks)[:, None, None]) & (
        slot[None, None, :] == jnp.arange(MOST)[None, :, None]
    )
    index = jnp.sum(hit * jnp.arange(number)[None, None, :], axis=2)
    valid = jnp.any(hit, axis=2)
    total = 0.0
    for s in range(MOST):
        picked = jnp.take(new_weight, index[:, s], axis=0)
        picked = jnp.where(valid[:, s][:, None, None], picked, jnp.zeros_like(picked))
        picked = picked.reshape(ranks, rows, groups, width // groups)
        total = total + jnp.einsum("bti,bigc->gbtc", cols, picked, preferred_element_type=f32)
    proj = (total * groups ** (-0.5)).astype(bf16)
    proj = proj.reshape(groups * ranks, count, width // groups)
    summed = lax.psum_scatter(proj, ("grp", "row"), scatter_dimension=0, tiled=True)[0]
    live = jnp.arange(count)[:, None] < counts[0]
    mixed = jnp.where(live, summed, jnp.zeros_like(summed))
    return (new_weight, mixed)


def solution(mesh):
    placed = (
        P("grp", "row", None),
        P("grp", "row", None),
        P("grp", None),
        P("row", None),
        P("row"),
    )
    return jax.shard_map(
        body,
        mesh=mesh,
        in_specs=placed,
        out_specs=(P("grp", "row", None), P("row", "grp")),
        check_vma=False,
    )
```

```python
import functools

import jax
import jax.numpy as jnp
from jax import lax
from jax.experimental import pallas as pl
from jax.experimental.pallas import tpu as pltpu
from jax.sharding import PartitionSpec as P

ITERS = 5
MOST = 2
CORES = 2

coef_a = 3.4445
coef_b = -4.775
coef_c = 2.0315
step_size = 0.5

f32 = jnp.float32
bf16 = jnp.bfloat16
MESH = pl.DeviceIdType.MESH


def far_first(n):
    return sorted(range(1, n), key=lambda k: abs(k - n // 2))


def greet(n, groups, grp_shifts):
    row, grp = lax.axis_index("row"), lax.axis_index("grp")
    barrier = pltpu.get_barrier_semaphore()
    for k in range(1, n):
        pl.semaphore_signal(
            barrier, inc=1, device_id=(grp, lax.rem(row + k, n)), device_id_type=MESH
        )
    for g in grp_shifts:
        pl.semaphore_signal(barrier, inc=1, device_id=(g, row), device_id_type=MESH)
    pl.semaphore_wait(barrier, n - 1 + len(grp_shifts))


def ortho_kernel(
    n, groups, raw, mine, back, cols, x, acc, gram, poly, ssem, rsem, tss, trs, gss, grs, bss, brs
):
    row, grp = lax.axis_index("row"), lax.axis_index("grp")
    width = raw.shape[2]
    others = [lax.rem(grp + k, groups) for k in range(1, groups)]
    greet(n, groups, others)
    order = far_first(n)

    def remote(src, dst, ss, rs, where):
        return pltpu.make_async_remote_copy(
            src_ref=src, dst_ref=dst, send_sem=ss, recv_sem=rs, device_id=where, device_id_type=MESH
        )

    sends, tsends = {}, {}
    for k in order:
        to = lax.rem(row + k, n)
        sends[k] = remote(raw.at[to], x.at[row], ssem.at[k], rsem.at[k], (grp, to))
        sends[k].start()
    for k in order:
        to = lax.rem(row + k, n)
        tsends[k] = remote(mine.at[to], cols.at[grp, row], tss.at[k], trs.at[k], (grp, to))
        tsends[k].start()

    def self_dot(v):
        return lax.dot_general(v, v, (((0,), (0,)), ((), ())), preferred_element_type=f32)

    x[row] = raw[row]
    cols[grp, row] = mine[row]
    acc[...] = self_dot(raw[row])
    for k in reversed(order):
        sends[k].wait_recv()
        acc[...] += self_dot(x[lax.rem(row + n - k, n)])

    total = acc[...]
    eye = lax.broadcasted_iota(jnp.int32, total.shape, 0) == lax.broadcasted_iota(
        jnp.int32, total.shape, 1
    )
    norm2 = jnp.sum(jnp.where(eye, total, 0.0), keepdims=True)
    scale = 1.0 / (jnp.sqrt(norm2) + 1e-07)
    acc[...] = jnp.where(norm2 < jnp.inf, scale * (scale * total), 0.0)

    gsends = []
    for turn in range(ITERS):
        first, last = turn == 0, turn == ITERS - 1
        gram[...] = acc[...].astype(bf16)
        square = jnp.dot(gram[...], gram[...], preferred_element_type=f32)
        poly[...] = (coef_b * gram[...].astype(f32) + coef_c * square).astype(bf16)

        def fresh(i):
            block = x[i]
            update = jnp.dot(block, poly[...], preferred_element_type=f32)
            if first:
                return ((coef_a * scale) * block.astype(f32) + scale * update).astype(bf16)
            return (coef_a * block.astype(f32) + update).astype(bf16)

        if not last:
            acc[...] = jnp.zeros_like(acc)

            def step(i, carry):
                block = fresh(i)
                x[i] = block
                acc[...] += self_dot(block)
                return carry

            lax.fori_loop(0, n, step, 0)
        if first:
            for k in order:
                tsends[k].wait_recv()
            for j, g in enumerate(others):
                copy = remote(cols.at[grp], cols.at[grp], gss.at[j], grs.at[j], (g, row))
                copy.start()
                gsends.append(copy)
        if last:
            bsends = {}
            for k in order:
                to = lax.rem(row + k, n)
                x[to] = fresh(to)
                bsends[k] = remote(x.at[to], back.at[row], bss.at[k], brs.at[k], (grp, to))
                bsends[k].start()
            back[row] = fresh(row)
    for k in order:
        sends[k].wait_send()
        tsends[k].wait_send()
    for copy in gsends:
        copy.wait()
    for k in order:
        bsends[k].wait()


def project_kernel(
    n, groups, index, valid, cols, fresh, out, part, got1, sum1, got2, sum2, got3,
    ss1, rs1, ss2, rs2, ss3, rs3
):
    row, grp = lax.axis_index("row"), lax.axis_index("grp")
    ys = groups // CORES
    y, core = grp // CORES, lax.rem(grp, CORES)
    count, piece = out.shape
    partners = [y * CORES + (1 - core)]
    partners += [lax.rem(y + j, ys) * CORES + core for j in range(1, ys)]
    greet(n, groups, partners)
    order = far_first(n) + [0]

    def remote(src, dst, ss, rs, where):
        copy = pltpu.make_async_remote_copy(
            src_ref=src, dst_ref=dst, send_sem=ss, recv_sem=rs, device_id=where, device_id_type=MESH
        )
        copy.start()
        return copy

    one, two, three = {}, {}, {}

    def stage1(k):
        b = lax.rem(row + k, n)
        tok = cols[:, b].reshape(count, cols.shape[3])
        total = jnp.zeros((count, groups * piece), f32)
        for s in range(MOST):
            term = jnp.dot(tok, fresh[index[b, s]], preferred_element_type=f32)
            total = total + jnp.where(valid[b, s] > 0, term, 0.0)
        total = (total * groups ** (-0.5)).astype(bf16)
        for g in range(groups):
            part[k, g % CORES, g // CORES] = total[:, g * piece : (g + 1) * piece]
        one[k] = remote(part.at[k, 1 - core], got1.at[k], ss1.at[k], rs1.at[k], (partners[0], row))

    def stage2(k):
        one[k].wait_recv()
        two[k] = []
        for j in range(1, ys):
            to = lax.rem(y + j, ys)
            both = part[k, core, to].astype(f32) + got1[k, to].astype(f32)
            sum1[k, j] = both.astype(bf16)
            two[k].append(
                remote(sum1.at[k, j], got2.at[k, j], ss2.at[k, j], rs2.at[k, j], (partners[j], row))
            )

    def stage3(k):
        total = part[k, core, y].astype(f32) + got1[k, y].astype(f32)
        for j in range(1, ys):
            two[k][j - 1].wait_recv()
            total = total + got2[k, j].astype(f32)
        if k == 0:
            return total
        sum2[k] = total.astype(bf16)
        to = lax.rem(row + k, n)
        three[k] = remote(sum2.at[k], got3.at[k], ss3.at[k], rs3.at[k], (grp, to))

    final = None
    lag2, lag3 = 1, 3
    for i in range(n + lag3):
        if i < n:
            stage1(order[i])
        if lag2 <= i < n + lag2:
            stage2(order[i - lag2])
        if lag3 <= i < n + lag3:
            final = stage3(order[i - lag3])
    for k in reversed(order[:-1]):
        three[k].wait_recv()
        final = final + got3[k].astype(f32)
    out[...] = final.astype(bf16)
    for k in order:
        one[k].wait_send()
        for copy in two[k]:
            copy.wait_send()
        if k:
            three[k].wait_send()


VM = pl.BlockSpec(memory_space=pltpu.VMEM)
SM = pl.BlockSpec(memory_space=pltpu.SMEM)


def body(grad, weight, owner, tokens, counts):
    ranks = lax.axis_size("row")
    groups = lax.axis_size("grp")
    number, rows, width = grad.shape
    assert number == ranks
    ys = groups // CORES
    dma = pltpu.SemaphoreType.DMA
    top = float(jnp.finfo(bf16).max)
    raw = jnp.clip(grad, -top, top).astype(bf16)

    count = tokens.shape[0]
    share = count // groups
    mine = lax.dynamic_slice_in_dim(tokens, lax.axis_index("grp") * share, share, 0)
    mine = jnp.stack([mine[:, r * rows : (r + 1) * rows] for r in range(ranks)])

    back, cols = pl.pallas_call(
        functools.partial(ortho_kernel, ranks, groups),
        out_shape=[
            jax.ShapeDtypeStruct((ranks, rows, width), bf16),
            jax.ShapeDtypeStruct((groups, ranks, share, rows), bf16),
        ],
        in_specs=[VM, VM],
        out_specs=[VM, VM],
        scratch_shapes=[
            pltpu.VMEM((ranks, rows, width), bf16),
            pltpu.VMEM((width, width), f32),
            pltpu.VMEM((width, width), bf16),
            pltpu.VMEM((width, width), bf16),
        ]
        + [dma((ranks,))] * 4
        + [dma((groups,))] * 2
        + [dma((ranks,))] * 2,
        compiler_params=pltpu.CompilerParams(
            collective_id=0, has_side_effects=True, vmem_limit_bytes=48 * 1024 * 1024
        ),
        name="ortho",
    )(raw, mine)
    new_weight = (weight.astype(f32) - step_size * back.astype(f32)).astype(bf16)

    target = owner[:, 0]
    before = jnp.arange(number)[None, :] < jnp.arange(number)[:, None]
    same = target[None, :] == target[:, None]
    slot = jnp.sum((same & before).astype(jnp.int32), axis=1)
    hit = (target[None, None, :] == jnp.arange(ranks)[:, None, None]) & (
        slot[None, None, :] == jnp.arange(MOST)[None, :, None]
    )
    index = jnp.sum(hit * jnp.arange(number)[None, None, :], axis=2).astype(jnp.int32)
    valid = jnp.any(hit, axis=2).astype(jnp.int32)

    piece = width // groups
    summed = pl.pallas_call(
        functools.partial(project_kernel, ranks, groups),
        out_shape=jax.ShapeDtypeStruct((count, piece), bf16),
        in_specs=[SM, SM, VM, VM],
        out_specs=VM,
        scratch_shapes=[
            pltpu.VMEM((ranks, CORES, ys, count, piece), bf16),
            pltpu.VMEM((ranks, ys, count, piece), bf16),
            pltpu.VMEM((ranks, ys, count, piece), bf16),
            pltpu.VMEM((ranks, ys, count, piece), bf16),
            pltpu.VMEM((ranks, count, piece), bf16),
            pltpu.VMEM((ranks, count, piece), bf16),
            dma((ranks,)),
            dma((ranks,)),
            dma((ranks, ys)),
            dma((ranks, ys)),
            dma((ranks,)),
            dma((ranks,)),
        ],
        compiler_params=pltpu.CompilerParams(
            collective_id=1, has_side_effects=True, vmem_limit_bytes=48 * 1024 * 1024
        ),
        name="project",
    )(index, valid, cols, new_weight)
    live = jnp.arange(count)[:, None] < counts[0]
    mixed = jnp.where(live, summed, jnp.zeros_like(summed))
    return (new_weight, mixed)


def solution(mesh):
    placed = (
        P("grp", "row", None),
        P("grp", "row", None),
        P("grp", None),
        P("row", None),
        P("row"),
    )
    return jax.shard_map(
        body,
        mesh=mesh,
        in_specs=placed,
        out_specs=(P("grp", "row", None), P("row", "grp")),
        check_vma=False,
    )
```

```python
import functools

import jax
import jax.numpy as jnp
from jax import lax
from jax.experimental import pallas as pl
from jax.experimental.pallas import tpu as pltpu
from jax.sharding import PartitionSpec as P

ITERS = 5
MOST = 2
CORES = 2

coef_a = 3.4445
coef_b = -4.775
coef_c = 2.0315
step_size = 0.5

f32 = jnp.float32
bf16 = jnp.bfloat16
MESH = pl.DeviceIdType.MESH


def far_first(n):
    return sorted(range(1, n), key=lambda k: abs(k - n // 2))


def greet(n, groups, grp_shifts):
    row, grp = lax.axis_index("row"), lax.axis_index("grp")
    barrier = pltpu.get_barrier_semaphore()
    for k in range(1, n):
        pl.semaphore_signal(
            barrier, inc=1, device_id=(grp, lax.rem(row + k, n)), device_id_type=MESH
        )
    for g in grp_shifts:
        pl.semaphore_signal(barrier, inc=1, device_id=(g, row), device_id_type=MESH)
    pl.semaphore_wait(barrier, n - 1 + len(grp_shifts))


def whole_kernel(
    n, groups, owner, index, valid, raw, tokens, weight, back, out, cols, x, acc, gram, poly,
    prod, part, got1, sum1, got2, sum2, got3,
    ssem, rsem, tss, trs, gss, grs, bss, brs, own_sem, ss1, rs1, ss2, rs2, ss3, rs3
):
    row, grp = lax.axis_index("row"), lax.axis_index("grp")
    width = raw.shape[2]
    others = [lax.rem(grp + k, groups) for k in range(1, groups)]
    greet(n, groups, others)
    order = far_first(n)

    def remote(src, dst, ss, rs, where):
        return pltpu.make_async_remote_copy(
            src_ref=src, dst_ref=dst, send_sem=ss, recv_sem=rs, device_id=where, device_id_type=MESH
        )

    def share_of(to):
        size, wide = cols.shape[2], cols.shape[3]
        down = pl.ds(pl.multiple_of(grp * size, size), size)
        return tokens.at[down, pl.ds(pl.multiple_of(to * wide, wide), wide)]

    sends, tsends = {}, {}
    for k in order:
        to = lax.rem(row + k, n)
        sends[k] = remote(raw.at[to], x.at[row], ssem.at[k], rsem.at[k], (grp, to))
        sends[k].start()
    for k in order:
        to = lax.rem(row + k, n)
        tsends[k] = remote(share_of(to), cols.at[grp, row], tss.at[k], trs.at[k], (grp, to))
        tsends[k].start()

    def self_dot(v):
        return lax.dot_general(v, v, (((0,), (0,)), ((), ())), preferred_element_type=f32)

    x[row] = raw[row]
    own = pltpu.make_async_copy(share_of(row), cols.at[grp, row], own_sem)
    own.start()
    acc[...] = self_dot(raw[row])
    for k in reversed(order):
        sends[k].wait_recv()
        acc[...] += self_dot(x[lax.rem(row + n - k, n)])

    total = acc[...]
    eye = lax.broadcasted_iota(jnp.int32, total.shape, 0) == lax.broadcasted_iota(
        jnp.int32, total.shape, 1
    )
    norm2 = jnp.sum(jnp.where(eye, total, 0.0), keepdims=True)
    scale = 1.0 / (jnp.sqrt(norm2) + 1e-07)
    acc[...] = jnp.where(norm2 < jnp.inf, scale * (scale * total), 0.0)

    gsends = []
    for turn in range(ITERS):
        first, last = turn == 0, turn == ITERS - 1
        gram[...] = acc[...].astype(bf16)
        square = jnp.dot(gram[...], gram[...], preferred_element_type=f32)
        poly[...] = (coef_b * gram[...].astype(f32) + coef_c * square).astype(bf16)

        def fresh(i):
            block = x[i]
            update = jnp.dot(block, poly[...], preferred_element_type=f32)
            if first:
                return ((coef_a * scale) * block.astype(f32) + scale * update).astype(bf16)
            return (coef_a * block.astype(f32) + update).astype(bf16)

        if not last:
            acc[...] = jnp.zeros_like(acc)

            def step(i, carry):
                block = fresh(i)
                x[i] = block
                acc[...] += self_dot(block)
                return carry

            lax.fori_loop(0, n, step, 0)
        if first:
            own.wait()
            for k in order:
                tsends[k].wait_recv()
            for j, g in enumerate(others):
                copy = remote(cols.at[grp], cols.at[grp], gss.at[j], grs.at[j], (g, row))
                copy.start()
                gsends.append(copy)
        if last:
            bsends = {}
            for k in order:
                to = lax.rem(row + k, n)
                x[to] = fresh(to)
                bsends[k] = remote(x.at[to], back.at[row], bss.at[k], brs.at[k], (grp, to))
                bsends[k].start()
            back[row] = fresh(row)
    for copy in gsends:
        copy.wait()

    def product(e):
        fresh = (weight[e].astype(f32) - step_size * back[e].astype(f32)).astype(bf16)
        tok = jnp.concatenate([cols[g, owner[e]] for g in range(groups)], axis=0)
        prod[e] = jnp.dot(tok, fresh, preferred_element_type=f32)

    product(row)
    for k in reversed(order):
        bsends[k].wait_recv()
        product(lax.rem(row + n - k, n))

    ys = groups // CORES
    y, core = grp // CORES, lax.rem(grp, CORES)
    count, piece = out.shape
    partners = [y * CORES + (1 - core)]
    partners += [lax.rem(y + j, ys) * CORES + core for j in range(1, ys)]
    turns = order + [0]

    def started(*args):
        copy = remote(*args)
        copy.start()
        return copy

    one, two, three = {}, {}, {}

    def stage1(k):
        b = lax.rem(row + k, n)
        total = jnp.zeros((count, groups * piece), f32)
        for s in range(MOST):
            total = total + jnp.where(valid[b, s] > 0, prod[index[b, s]], 0.0)
        total = (total * groups ** (-0.5)).astype(bf16)
        for g in range(groups):
            part[k, g % CORES, g // CORES] = total[:, g * piece : (g + 1) * piece]
        one[k] = started(part.at[k, 1 - core], got1.at[k], ss1.at[k], rs1.at[k], (partners[0], row))

    def stage2(k):
        one[k].wait_recv()
        two[k] = []
        for j in range(1, ys):
            to = lax.rem(y + j, ys)
            both = part[k, core, to].astype(f32) + got1[k, to].astype(f32)
            sum1[k, j] = both.astype(bf16)
            two[k].append(
                started(sum1.at[k, j], got2.at[k, j], ss2.at[k, j], rs2.at[k, j], (partners[j], row))
            )

    def stage3(k):
        total = part[k, core, y].astype(f32) + got1[k, y].astype(f32)
        for j in range(1, ys):
            two[k][j - 1].wait_recv()
            total = total + got2[k, j].astype(f32)
        if k == 0:
            return total
        sum2[k] = total.astype(bf16)
        to = lax.rem(row + k, n)
        three[k] = started(sum2.at[k], got3.at[k], ss3.at[k], rs3.at[k], (grp, to))

    final = None
    lag2, lag3 = 1, 3
    for i in range(n + lag3):
        if i < n:
            stage1(turns[i])
        if lag2 <= i < n + lag2:
            stage2(turns[i - lag2])
        if lag3 <= i < n + lag3:
            final = stage3(turns[i - lag3])
    for k in reversed(turns[:-1]):
        three[k].wait_recv()
        final = final + got3[k].astype(f32)
    out[...] = final.astype(bf16)
    for k in turns:
        one[k].wait_send()
        for copy in two[k]:
            copy.wait_send()
        if k:
            three[k].wait_send()
    for k in order:
        sends[k].wait_send()
        tsends[k].wait_send()
        bsends[k].wait_send()


VM = pl.BlockSpec(memory_space=pltpu.VMEM)
SM = pl.BlockSpec(memory_space=pltpu.SMEM)


def body(grad, weight, owner, tokens, counts):
    ranks = lax.axis_size("row")
    groups = lax.axis_size("grp")
    number, rows, width = grad.shape
    assert number == ranks
    ys = groups // CORES
    dma = pltpu.SemaphoreType.DMA
    top = float(jnp.finfo(bf16).max)
    raw = jnp.clip(grad, -top, top).astype(bf16)

    count = tokens.shape[0]
    share = count // groups
    target = owner[:, 0]
    before = jnp.arange(number)[None, :] < jnp.arange(number)[:, None]
    same = target[None, :] == target[:, None]
    slot = jnp.sum((same & before).astype(jnp.int32), axis=1)
    hit = (target[None, None, :] == jnp.arange(ranks)[:, None, None]) & (
        slot[None, None, :] == jnp.arange(MOST)[None, :, None]
    )
    index = jnp.sum(hit * jnp.arange(number)[None, None, :], axis=2).astype(jnp.int32)
    valid = jnp.any(hit, axis=2).astype(jnp.int32)

    piece = width // groups
    back, summed = pl.pallas_call(
        functools.partial(whole_kernel, ranks, groups),
        out_shape=[
            jax.ShapeDtypeStruct((ranks, rows, width), bf16),
            jax.ShapeDtypeStruct((count, piece), bf16),
        ],
        in_specs=[SM, SM, SM, VM, pl.BlockSpec(memory_space=pl.ANY), VM],
        out_specs=[VM, VM],
        scratch_shapes=[
            pltpu.VMEM((groups, ranks, share, rows), bf16),
            pltpu.VMEM((ranks, rows, width), bf16),
            pltpu.VMEM((width, width), f32),
            pltpu.VMEM((width, width), bf16),
            pltpu.VMEM((width, width), bf16),
            pltpu.VMEM((ranks, count, width), f32),
            pltpu.VMEM((ranks, CORES, ys, count, piece), bf16),
            pltpu.VMEM((ranks, ys, count, piece), bf16),
            pltpu.VMEM((ranks, ys, count, piece), bf16),
            pltpu.VMEM((ranks, ys, count, piece), bf16),
            pltpu.VMEM((ranks, count, piece), bf16),
            pltpu.VMEM((ranks, count, piece), bf16),
        ]
        + [dma((ranks,))] * 4
        + [dma((groups,))] * 2
        + [dma((ranks,))] * 2
        + [dma]
        + [dma((ranks,))] * 2
        + [dma((ranks, ys))] * 2
        + [dma((ranks,))] * 2,
        compiler_params=pltpu.CompilerParams(
            collective_id=0, has_side_effects=True, vmem_limit_bytes=60 * 1024 * 1024
        ),
        name="whole",
    )(target, index, valid, raw, tokens, weight)
    new_weight = (weight.astype(f32) - step_size * back.astype(f32)).astype(bf16)
    live = jnp.arange(count)[:, None] < counts[0]
    mixed = jnp.where(live, summed, jnp.zeros_like(summed))
    return (new_weight, mixed)


def solution(mesh):
    placed = (
        P("grp", "row", None),
        P("grp", "row", None),
        P("grp", None),
        P("row", None),
        P("row"),
    )
    return jax.shard_map(
        body,
        mesh=mesh,
        in_specs=placed,
        out_specs=(P("grp", "row", None), P("row", "grp")),
        check_vma=False,
    )
```

```python
import functools

import jax
import jax.numpy as jnp
from jax import lax
from jax.experimental import pallas as pl
from jax.experimental.pallas import tpu as pltpu
from jax.sharding import PartitionSpec as P

ITERS = 5
MOST = 2
CORES = 2
LAGS = (1, 3)

coef_a = 3.4445
coef_b = -4.775
coef_c = 2.0315
step_size = 0.5

f32 = jnp.float32
bf16 = jnp.bfloat16
MESH = pl.DeviceIdType.MESH


def far_first(n):
    return sorted(range(1, n), key=lambda k: abs(k - n // 2))


def greet(n, groups, grp_shifts):
    row, grp = lax.axis_index("row"), lax.axis_index("grp")
    barrier = pltpu.get_barrier_semaphore()
    for k in range(1, n):
        pl.semaphore_signal(
            barrier, inc=1, device_id=(grp, lax.rem(row + k, n)), device_id_type=MESH
        )
    for g in grp_shifts:
        pl.semaphore_signal(barrier, inc=1, device_id=(g, row), device_id_type=MESH)
    pl.semaphore_wait(barrier, n - 1 + len(grp_shifts))


def ortho_kernel(
    n, groups, raw, tokens, back, cols, x, acc, gram, poly, ssem, rsem, tss, trs, gss, grs, bss, brs, own_sem
):
    row, grp = lax.axis_index("row"), lax.axis_index("grp")
    width = raw.shape[2]
    others = [lax.rem(grp + k, groups) for k in range(1, groups)]
    greet(n, groups, others)
    order = far_first(n)

    def remote(src, dst, ss, rs, where):
        return pltpu.make_async_remote_copy(
            src_ref=src, dst_ref=dst, send_sem=ss, recv_sem=rs, device_id=where, device_id_type=MESH
        )

    def share_of(to):
        size, wide = cols.shape[2], cols.shape[3]
        down = pl.ds(pl.multiple_of(grp * size, size), size)
        return tokens.at[down, pl.ds(pl.multiple_of(to * wide, wide), wide)]

    sends, tsends = {}, {}
    for k in order:
        to = lax.rem(row + k, n)
        sends[k] = remote(raw.at[to], x.at[row], ssem.at[k], rsem.at[k], (grp, to))
        sends[k].start()
    for k in order:
        to = lax.rem(row + k, n)
        tsends[k] = remote(share_of(to), cols.at[grp, row], tss.at[k], trs.at[k], (grp, to))
        tsends[k].start()

    def self_dot(v):
        return lax.dot_general(v, v, (((0,), (0,)), ((), ())), preferred_element_type=f32)

    x[row] = raw[row]
    own = pltpu.make_async_copy(share_of(row), cols.at[grp, row], own_sem)
    own.start()
    acc[...] = self_dot(raw[row])
    for k in reversed(order):
        sends[k].wait_recv()
        acc[...] += self_dot(x[lax.rem(row + n - k, n)])

    total = acc[...]
    eye = lax.broadcasted_iota(jnp.int32, total.shape, 0) == lax.broadcasted_iota(
        jnp.int32, total.shape, 1
    )
    norm2 = jnp.sum(jnp.where(eye, total, 0.0), keepdims=True)
    scale = 1.0 / (jnp.sqrt(norm2) + 1e-07)
    acc[...] = jnp.where(norm2 < jnp.inf, scale * (scale * total), 0.0)

    gsends = []
    for turn in range(ITERS):
        first, last = turn == 0, turn == ITERS - 1
        gram[...] = acc[...].astype(bf16)
        square = jnp.dot(gram[...], gram[...], preferred_element_type=f32)
        poly[...] = (coef_b * gram[...].astype(f32) + coef_c * square).astype(bf16)

        def fresh(i):
            block = x[i]
            update = jnp.dot(block, poly[...], preferred_element_type=f32)
            if first:
                return ((coef_a * scale) * block.astype(f32) + scale * update).astype(bf16)
            return (coef_a * block.astype(f32) + update).astype(bf16)

        if not last:
            acc[...] = jnp.zeros_like(acc)

            def step(i, carry):
                block = fresh(i)
                x[i] = block
                acc[...] += self_dot(block)
                return carry

            lax.fori_loop(0, n, step, 0)
        if first:
            own.wait()
            for k in order:
                tsends[k].wait_recv()
            for j, g in enumerate(others):
                copy = remote(cols.at[grp], cols.at[grp], gss.at[j], grs.at[j], (g, row))
                copy.start()
                gsends.append(copy)
        if last:
            bsends = {}
            for k in order:
                to = lax.rem(row + k, n)
                x[to] = fresh(to)
                bsends[k] = remote(x.at[to], back.at[row], bss.at[k], brs.at[k], (grp, to))
                bsends[k].start()
            back[row] = fresh(row)
    for k in order:
        sends[k].wait_send()
        tsends[k].wait_send()
    for copy in gsends:
        copy.wait()
    for k in order:
        bsends[k].wait()


def project_kernel(
    n, groups, index, valid, cols, fresh, out, part, got1, sum1, got2, sum2, got3,
    ss1, rs1, ss2, rs2, ss3, rs3
):
    row, grp = lax.axis_index("row"), lax.axis_index("grp")
    ys = groups // CORES
    y, core = grp // CORES, lax.rem(grp, CORES)
    count, piece = out.shape
    partners = [y * CORES + (1 - core)]
    partners += [lax.rem(y + j, ys) * CORES + core for j in range(1, ys)]
    greet(n, groups, partners)
    order = far_first(n) + [0]

    def remote(src, dst, ss, rs, where):
        copy = pltpu.make_async_remote_copy(
            src_ref=src, dst_ref=dst, send_sem=ss, recv_sem=rs, device_id=where, device_id_type=MESH
        )
        copy.start()
        return copy

    one, two, three = {}, {}, {}

    def stage1(k):
        b = lax.rem(row + k, n)
        tok = cols[:, b].reshape(count, cols.shape[3])
        total = jnp.zeros((count, groups * piece), f32)
        for s in range(MOST):
            term = jnp.dot(tok, fresh[index[b, s]], preferred_element_type=f32)
            total = total + jnp.where(valid[b, s] > 0, term, 0.0)
        total = (total * groups ** (-0.5)).astype(bf16)
        for g in range(groups):
            part[k, g % CORES, g // CORES] = total[:, g * piece : (g + 1) * piece]
        one[k] = remote(part.at[k, 1 - core], got1.at[k], ss1.at[k], rs1.at[k], (partners[0], row))

    def stage2(k):
        one[k].wait_recv()
        two[k] = []
        for j in range(1, ys):
            to = lax.rem(y + j, ys)
            both = part[k, core, to].astype(f32) + got1[k, to].astype(f32)
            sum1[k, j] = both.astype(bf16)
            two[k].append(
                remote(sum1.at[k, j], got2.at[k, j], ss2.at[k, j], rs2.at[k, j], (partners[j], row))
            )

    def stage3(k):
        total = part[k, core, y].astype(f32) + got1[k, y].astype(f32)
        for j in range(1, ys):
            two[k][j - 1].wait_recv()
            total = total + got2[k, j].astype(f32)
        if k == 0:
            return total
        sum2[k] = total.astype(bf16)
        to = lax.rem(row + k, n)
        three[k] = remote(sum2.at[k], got3.at[k], ss3.at[k], rs3.at[k], (grp, to))

    final = None
    lag2, lag3 = LAGS
    for i in range(n + lag3):
        if i < n:
            stage1(order[i])
        if lag2 <= i < n + lag2:
            stage2(order[i - lag2])
        if lag3 <= i < n + lag3:
            final = stage3(order[i - lag3])
    for k in reversed(order[:-1]):
        three[k].wait_recv()
        final = final + got3[k].astype(f32)
    out[...] = final.astype(bf16)
    for k in order:
        one[k].wait_send()
        for copy in two[k]:
            copy.wait_send()
        if k:
            three[k].wait_send()


VM = pl.BlockSpec(memory_space=pltpu.VMEM)
SM = pl.BlockSpec(memory_space=pltpu.SMEM)


def body(grad, weight, owner, tokens, counts):
    ranks = lax.axis_size("row")
    groups = lax.axis_size("grp")
    number, rows, width = grad.shape
    assert number == ranks
    ys = groups // CORES
    dma = pltpu.SemaphoreType.DMA
    top = float(jnp.finfo(bf16).max)
    raw = jnp.clip(grad, -top, top).astype(bf16)

    count = tokens.shape[0]
    share = count // groups
    back, cols = pl.pallas_call(
        functools.partial(ortho_kernel, ranks, groups),
        out_shape=[
            jax.ShapeDtypeStruct((ranks, rows, width), bf16),
            jax.ShapeDtypeStruct((groups, ranks, share, rows), bf16),
        ],
        in_specs=[VM, pl.BlockSpec(memory_space=pl.ANY)],
        out_specs=[VM, VM],
        scratch_shapes=[
            pltpu.VMEM((ranks, rows, width), bf16),
            pltpu.VMEM((width, width), f32),
            pltpu.VMEM((width, width), bf16),
            pltpu.VMEM((width, width), bf16),
        ]
        + [dma((ranks,))] * 4
        + [dma((groups,))] * 2
        + [dma((ranks,))] * 2
        + [dma],
        compiler_params=pltpu.CompilerParams(
            collective_id=0, has_side_effects=True, vmem_limit_bytes=48 * 1024 * 1024
        ),
        name="ortho",
    )(raw, tokens)
    new_weight = (weight.astype(f32) - step_size * back.astype(f32)).astype(bf16)

    target = owner[:, 0]
    before = jnp.arange(number)[None, :] < jnp.arange(number)[:, None]
    same = target[None, :] == target[:, None]
    slot = jnp.sum((same & before).astype(jnp.int32), axis=1)
    hit = (target[None, None, :] == jnp.arange(ranks)[:, None, None]) & (
        slot[None, None, :] == jnp.arange(MOST)[None, :, None]
    )
    index = jnp.sum(hit * jnp.arange(number)[None, None, :], axis=2).astype(jnp.int32)
    valid = jnp.any(hit, axis=2).astype(jnp.int32)

    piece = width // groups
    summed = pl.pallas_call(
        functools.partial(project_kernel, ranks, groups),
        out_shape=jax.ShapeDtypeStruct((count, piece), bf16),
        in_specs=[SM, SM, VM, VM],
        out_specs=VM,
        scratch_shapes=[
            pltpu.VMEM((ranks, CORES, ys, count, piece), bf16),
            pltpu.VMEM((ranks, ys, count, piece), bf16),
            pltpu.VMEM((ranks, ys, count, piece), bf16),
            pltpu.VMEM((ranks, ys, count, piece), bf16),
            pltpu.VMEM((ranks, count, piece), bf16),
            pltpu.VMEM((ranks, count, piece), bf16),
            dma((ranks,)),
            dma((ranks,)),
            dma((ranks, ys)),
            dma((ranks, ys)),
            dma((ranks,)),
            dma((ranks,)),
        ],
        compiler_params=pltpu.CompilerParams(
            collective_id=1, has_side_effects=True, vmem_limit_bytes=48 * 1024 * 1024
        ),
        name="project",
    )(index, valid, cols, new_weight)
    live = jnp.arange(count)[:, None] < counts[0]
    mixed = jnp.where(live, summed, jnp.zeros_like(summed))
    return (new_weight, mixed)


def solution(mesh):
    placed = (
        P("grp", "row", None),
        P("grp", "row", None),
        P("grp", None),
        P("row", None),
        P("row"),
    )
    return jax.shard_map(
        body,
        mesh=mesh,
        in_specs=placed,
        out_specs=(P("grp", "row", None), P("row", "grp")),
        check_vma=False,
    )
```
